512 devices in a mesh: ctx: 128 (over y, z, core), head: 4 (over x).
Axes of the slice: x: 4, y: 8, z: 8, core: 2. Of those that a mesh axis runs over, the one named last changes fastest.
Arguments:
- tokens: bfloat16 [2, 16384, 4096], P(None, 'ctx', 'head'), may hold values from -6 to 6
- w_query: bfloat16 [4096, 2048], P('ctx', 'head'), may hold values from -0.09375 to 0.09375
- w_key: bfloat16 [4096, 2048], P('ctx', 'head'), may hold values from -0.09375 to 0.09375
- w_value: bfloat16 [4096, 2048], P('ctx', 'head'), may hold values from -0.09375 to 0.09375
- norm_gain: float32 [2048], P('head'), may hold values from 0.1 to 1.9
Outputs:
- attended: bfloat16 [2, 16384, 2048], P(None, 'ctx', 'head')
The draws below stay inside these ranges and needn't reach their ends.
All inputs are finite; a program needn't handle non-finite values.
Results may differ from the reference program's by a relative error of at most 0.0072.
Values may be sent and summed in bfloat16 or wider, within the bound.
No kernel may reach another device: no remote copies, remote signals or barrier semaphores. Data moves between devices by JAX's collectives and lax.ppermute only.
A program may use at most 192 MiB of HBM per device.

```python
import jax
import jax.numpy as jnp
from jax import lax

D = 4096
HD = 128
HEADS = 16
SEQS = 2
SPAN = 128
LENGTH = 16384


def shard_levels(rng, dims, cuts, least, largest):
    loudness = 1.0
    for axis_at, parts in cuts:
        draws = jax.random.uniform(jax.random.fold_in(jax.random.fold_in(rng, 6), axis_at), (parts,), jnp.float32, least / len(cuts), largest / len(cuts))
        loudness = loudness * jnp.repeat(jnp.exp(draws), dims[axis_at] // parts).reshape((-1,) + (1,) * (len(dims) - 1 - axis_at))
    return loudness


def gaussian(stream_key, dims, deviation, reach, pieces=(), dtype=jnp.bfloat16):
    result = jax.random.normal(stream_key, dims, jnp.float32) * deviation
    if len(pieces) > 0:
        result = shard_levels(stream_key, dims, pieces, -0.22, 0.18) * result
    return jnp.clip(result, min=-reach, max=reach).astype(dtype)


def setup_inputs(seed: int = 0) -> dict:
    keys = jax.random.split(jax.random.key(seed), 6)
    tokens = gaussian(keys[0], (SEQS, LENGTH, D), 1.0, 6.0, ((1, 128), (2, 4)))
    w_query = gaussian(keys[1], (D, HEADS * HD), D ** -0.5, 0.09375, ((0, 128), (1, 4)))
    w_key = gaussian(keys[2], (D, HEADS * HD), D ** -0.5, 0.09375, ((0, 128), (1, 4)))
    w_value = gaussian(keys[3], (D, HEADS * HD), D ** -0.5, 0.09375, ((0, 128), (1, 4)))
    norm_gain = jnp.clip(1.0 + 0.18 * jax.random.normal(keys[4], (HEADS * HD,), jnp.float32), 0.1, 1.9)
    return {"tokens": tokens, "w_query": w_query, "w_key": w_key, "w_value": w_value, "norm_gain": norm_gain}


def rounded(values):
    return lax.optimization_barrier(values.astype(jnp.bfloat16)).astype(jnp.float32)

def reference(tokens, w_query, w_key, w_value, norm_gain):
    token_rows = tokens.reshape(SEQS * LENGTH, D)
    blocks = LENGTH // SPAN

    def project(weight, gated):
        product = jnp.dot(token_rows, weight, preferred_element_type=jnp.float32)
        if gated:
            product = jax.nn.silu(product)
        product = product.astype(jnp.bfloat16).reshape(SEQS, blocks, SPAN, HEADS, HD)
        return product.transpose(1, 0, 3, 2, 4)
    query = project(w_query, True)
    key_all = project(w_key, True)
    value_all = project(w_value, False)
    positions = jnp.arange(SPAN)
    causal = positions[:, None] >= positions[None, :]
    gain_view = norm_gain.reshape(1, HEADS, 1, HD)

    def advance(carried, inputs):
        query_blk, key_blk, value_blk = inputs
        query_f = query_blk.astype(jnp.float32)
        key_f = key_blk.astype(jnp.float32)
        value_f = value_blk.astype(jnp.float32)
        scores = jnp.einsum('shtd,shud->shtu', query_f, key_f)
        masked = rounded(jnp.where(causal, scores, 0.0))
        local_out = jnp.einsum('shtu,shud->shtd', masked, value_f)
        from_prefix = jnp.einsum('shtd,shde->shte', query_f, rounded(carried))
        total = local_out + from_prefix
        scale_inv = lax.rsqrt(lax.optimization_barrier(jnp.mean(total * total, axis=-1, keepdims=True)) + 1e-06)
        normed = (total * scale_inv * gain_view).astype(jnp.bfloat16)
        states = jnp.einsum('shud,shue->shde', key_f, value_f)
        return (carried + states, normed)
    initial = jnp.zeros((SEQS, HEADS, HD, HD), jnp.float32)
    _, outputs = lax.scan(advance, initial, (query, key_all, value_all))
    return outputs.transpose(1, 0, 3, 2, 4).reshape(SEQS, LENGTH, HEADS * HD)
```

```python
import jax
import jax.numpy as jnp
from jax import lax
from jax.experimental import pallas as pl
from jax.experimental.pallas import tpu as pltpu
from jax.sharding import PartitionSpec as P

HD = 128


def scan_kernel(states_ref, prefix_ref):
    count = states_ref.shape[0]

    def one(block, carried):
        prefix_ref[block] = carried.astype(prefix_ref.dtype)
        return carried + states_ref[block]

    lax.fori_loop(0, count, one, jnp.zeros(states_ref.shape[1:], jnp.float32))


def exclusive(slices):
    return pl.pallas_call(
        scan_kernel,
        out_shape=jax.ShapeDtypeStruct(slices.shape, jnp.bfloat16),
        in_specs=[pl.BlockSpec(memory_space=pltpu.VMEM)],
        out_specs=pl.BlockSpec(memory_space=pltpu.VMEM),
    )(slices)


def body(tokens, w_query, w_key, w_value, norm_gain, *, ctx, heads):
    seq_count, span_len, shard = tokens.shape
    features = w_query.shape[1]
    head_count = features // HD
    rows = seq_count * span_len
    weights = jnp.concatenate([w_query, w_key, w_value], axis=1)
    full = lax.all_gather(weights, "ctx", axis=0, tiled=True)
    place = lax.axis_index("head")
    own = tokens.reshape(rows, shard)
    token_rows = jnp.zeros((rows, shard * heads), tokens.dtype)
    token_rows = lax.dynamic_update_slice(token_rows, own, (0, place * shard))
    for hop in range(1, heads):
        ring = [(i, (i + hop) % heads) for i in range(heads)]
        came = lax.ppermute(own, "head", ring)
        source = lax.rem(place + heads - hop, heads)
        token_rows = lax.dynamic_update_slice(token_rows, came, (0, source * shard))
    sums = jnp.dot(token_rows, full, preferred_element_type=jnp.float32)

    def heads_first(projected):
        shaped = projected.astype(jnp.bfloat16).reshape(seq_count, span_len, head_count, HD)
        return shaped.transpose(0, 2, 1, 3)

    query = heads_first(jax.nn.silu(sums[:, :features]))
    key_all = heads_first(jax.nn.silu(sums[:, features : 2 * features]))
    value_all = heads_first(sums[:, 2 * features :])
    states = jnp.einsum("shud,shue->shde", key_all, value_all, preferred_element_type=jnp.float32)
    slices = lax.all_to_all(states.reshape(ctx, -1, HD), "ctx", 0, 0, tiled=True)
    prefix = lax.all_to_all(exclusive(slices), "ctx", 0, 0, tiled=True)
    prefix = prefix.reshape(states.shape)
    positions = jnp.arange(span_len)
    causal = positions[:, None] >= positions[None, :]
    scores = jnp.einsum("shtd,shud->shtu", query, key_all, preferred_element_type=jnp.float32)
    masked = jnp.where(causal, scores, 0.0).astype(jnp.bfloat16)
    local_out = jnp.einsum("shtu,shud->shtd", masked, value_all, preferred_element_type=jnp.float32)
    from_prefix = jnp.einsum("shtd,shde->shte", query, prefix, preferred_element_type=jnp.float32)
    total = local_out + from_prefix
    scale_inv = lax.rsqrt(jnp.mean(total * total, axis=-1, keepdims=True) + 1e-06)
    gain_view = norm_gain.reshape(1, head_count, 1, HD)
    normed = total * scale_inv * gain_view
    return normed.transpose(0, 2, 1, 3).reshape(seq_count, span_len, features).astype(jnp.bfloat16)


def solution(mesh):
    sizes = dict(mesh.shape)
    in_specs = (P(None, "ctx", "head"), P("ctx", "head"), P("ctx", "head"), P("ctx", "head"), P("head"))

    def step(*operands):
        return body(*operands, ctx=sizes["ctx"], heads=sizes["head"])

    return jax.shard_map(step, mesh=mesh, in_specs=in_specs, out_specs=P(None, "ctx", "head"), check_vma=False)
```

```python
import jax
import jax.numpy as jnp
from jax import lax
from jax.experimental import pallas as pl
from jax.experimental.pallas import tpu as pltpu
from jax.sharding import PartitionSpec as P


HD = 128
SIDE = 8
CORES = 2


def index(y, z, core):
    return ((y % SIDE) * SIDE + z % SIDE) * CORES + core


def everyone():
    return [(y, z, core) for y in range(SIDE) for z in range(SIDE) for core in range(CORES)]


def across():
    return [(index(y, z, core), index(y, z, 1 - core)) for y, z, core in everyone()]


def along_second(hop):
    return [
        (index(y, z, core), index(y + hop, z, core) if core == 0 else index(y, z + hop, core))
        for y, z, core in everyone()
    ]


def first_groups():
    groups = [[index(y, z, 0) for z in range(SIDE)] for y in range(SIDE)]
    return groups + [[index(y, z, 1) for y in range(SIDE)] for z in range(SIDE)]


def chip_groups():
    return [[index(y, z, core) for y in range(SIDE) for z in range(SIDE)] for core in range(CORES)]


def block_at(number, second):
    far = (number + 1) // 2
    return jnp.where(number % 2 == 1, second + SIDE - far, second + far) % SIDE


def multiply(info_ref, piece_refs, block_refs, lhs, rhs, total, lhs_sems, rhs_sems, first):
    core, second, head_at = info_ref[0], info_ref[1], info_ref[2]
    heads, count = len(piece_refs), len(block_refs)
    steps = rhs.shape[1] // HD
    lhs_copies = [pltpu.make_async_copy(r, lhs.at[i], lhs_sems.at[i]) for i, r in enumerate(piece_refs)]
    rhs_copies = [pltpu.make_async_copy(r, rhs.at[i], rhs_sems.at[i]) for i, r in enumerate(block_refs)]
    rhs_copies[0].start()
    for copy in lhs_copies:
        copy.start()
    for copy in rhs_copies[1:]:
        copy.start()
    for copy in lhs_copies:
        copy.wait()
    group = 2 * HD

    def one(number, _):
        pltpu.make_async_copy(block_refs[0], rhs.at[number], rhs_sems.at[number]).wait()
        at = block_at(first + number, second)
        left = []
        for p in range(steps):
            part = jnp.where(core == 0, at // 2, p)
            hop = (head_at + heads - part) % heads
            lane = jnp.where(core == 0, (at % 2) * steps + p, at)
            left.append(lhs[hop, :, pl.ds(pl.multiple_of(lane * HD, HD), HD)])
        left = jnp.concatenate(left, axis=1)
        for g in range(total.shape[1] // group):
            cols = slice(g * group, (g + 1) * group)
            total[:, cols] += jnp.dot(left, rhs[number, :, cols], preferred_element_type=jnp.float32)
        return 0

    lax.fori_loop(0, count, one, 0)


def early_kernel(heads, count, info_ref, *refs):
    pieces, blocks = refs[:heads], refs[heads : heads + count]
    out, lhs, rhs, lhs_sems, rhs_sems = refs[heads + count :]
    out[...] = jnp.zeros_like(out)
    multiply(info_ref, pieces, blocks, lhs, rhs, out, lhs_sems, rhs_sems, 0)


def late_kernel(heads, count, first, seqs, info_ref, *refs):
    pieces, blocks = refs[:heads], refs[heads : heads + count]
    sums, qkv, states, lhs, rhs, total, lhs_sems, rhs_sems = refs[heads + count :]
    total[...] = sums[...]
    multiply(info_ref, pieces, blocks, lhs, rhs, total, lhs_sems, rhs_sems, first)
    half = total.shape[1] // 3
    gated = total[:, : 2 * half]
    qkv[:, : 2 * half] = (gated / (1.0 + jnp.exp(-gated))).astype(qkv.dtype)
    qkv[:, 2 * half :] = total[:, 2 * half :].astype(qkv.dtype)
    span = total.shape[0] // (CORES * seqs)
    for s in range(seqs):
        for h in range(half // HD):
            acc = jnp.zeros((HD, HD), jnp.float32)
            for c in range(CORES):
                at = pl.ds((c * seqs + s) * span, span)
                key = qkv[at, pl.ds(half + h * HD, HD)]
                value = qkv[at, pl.ds(2 * half + h * HD, HD)]
                acc += lax.dot_general(key, value, (((0,), (0,)), ((), ())), preferred_element_type=jnp.float32)
            states[s, h] = acc


def call_info(core, second, head_at):
    return jnp.stack([core, second, head_at]).astype(jnp.int32)


SMEM = pl.BlockSpec(memory_space=pltpu.SMEM)
ANY = pl.BlockSpec(memory_space=pl.ANY)
VMEM = pl.BlockSpec(memory_space=pltpu.VMEM)


def early_product(info, pieces, blocks):
    rows, columns = pieces[0].shape[0], blocks[0].shape[1]
    heads, count = len(pieces), len(blocks)

    def kernel(*refs):
        early_kernel(heads, count, *refs)

    return pl.pallas_call(
        kernel,
        out_shape=jax.ShapeDtypeStruct((rows, columns), jnp.float32),
        in_specs=[SMEM] + [ANY] * (heads + count),
        out_specs=VMEM,
        scratch_shapes=[
            pltpu.VMEM((heads,) + pieces[0].shape, pieces[0].dtype),
            pltpu.VMEM((count,) + blocks[0].shape, blocks[0].dtype),
            pltpu.SemaphoreType.DMA((heads,)),
            pltpu.SemaphoreType.DMA((count,)),
        ],
        cost_estimate=pl.CostEstimate(
            flops=2 * rows * columns * blocks[0].shape[0] * count, bytes_accessed=8 << 20, transcendentals=0
        ),
    )(info, *pieces, *blocks)


def late_product(info, pieces, blocks, sums, first, seqs):
    rows, columns = sums.shape
    heads, count = len(pieces), len(blocks)

    def kernel(*refs):
        late_kernel(heads, count, first, seqs, *refs)

    return pl.pallas_call(
        kernel,
        out_shape=(
            jax.ShapeDtypeStruct((rows, columns), jnp.bfloat16),
            jax.ShapeDtypeStruct((seqs, columns // 3 // HD, HD, HD), jnp.float32),
        ),
        in_specs=[SMEM] + [ANY] * (heads + count) + [VMEM],
        out_specs=(VMEM, VMEM),
        scratch_shapes=[
            pltpu.VMEM((heads,) + pieces[0].shape, pieces[0].dtype),
            pltpu.VMEM((count,) + blocks[0].shape, blocks[0].dtype),
            pltpu.VMEM((rows, columns), jnp.float32),
            pltpu.SemaphoreType.DMA((heads,)),
            pltpu.SemaphoreType.DMA((count,)),
        ],
        cost_estimate=pl.CostEstimate(
            flops=2 * rows * columns * blocks[0].shape[0] * count, bytes_accessed=8 << 20, transcendentals=0
        ),
    )(info, *pieces, *blocks, sums)


def scan_kernel(slices_ref, prefix_ref):
    def one(block, carried):
        prefix_ref[block] = carried.astype(prefix_ref.dtype)
        return carried + slices_ref[block]

    lax.fori_loop(0, slices_ref.shape[0], one, jnp.zeros(slices_ref.shape[1:], jnp.float32), unroll=8)


def exclusive(slices):
    return pl.pallas_call(
        scan_kernel,
        out_shape=jax.ShapeDtypeStruct(slices.shape, jnp.bfloat16),
        in_specs=[VMEM],
        out_specs=VMEM,
    )(slices)


def attend_kernel(seqs, info_ref, qkv, prefix, gain, mine, other, spans):
    half = qkv.shape[1] // 3
    span = qkv.shape[0] // (CORES * seqs)
    both = CORES * span
    ahead = lax.broadcasted_iota(jnp.int32, (both, both), 0)
    causal = ahead >= lax.broadcasted_iota(jnp.int32, (both, both), 1)
    for s in range(seqs):
        for h in range(half // HD):

            def chosen(kind):
                lanes = pl.ds(kind * half + h * HD, HD)
                return jnp.concatenate([qkv[pl.ds((c * seqs + s) * span, span), lanes] for c in range(CORES)], axis=0)

            query, key, value = chosen(0), chosen(1), chosen(2)
            scores = lax.dot_general(query, key, (((1,), (1,)), ((), ())), preferred_element_type=jnp.float32)
            masked = jnp.where(causal, scores, 0.0).astype(jnp.bfloat16)
            total = jnp.dot(masked, value, preferred_element_type=jnp.float32)
            total += jnp.dot(query, prefix[s, h], preferred_element_type=jnp.float32)
            scale_inv = lax.rsqrt(jnp.mean(total * total, axis=-1, keepdims=True) + 1e-06)
            normed = (total * scale_inv * gain[:, pl.ds(h * HD, HD)]).astype(mine.dtype)
            for c in range(CORES):
                spans[c, s, :, pl.ds(h * HD, HD)] = normed[c * span : (c + 1) * span]
    core = info_ref[0]
    mine[...] = spans[core]
    other[...] = spans[1 - core]


def attend(info, qkv, prefix, gain, seqs):
    rows, columns = qkv.shape
    shape = (seqs, rows // CORES // seqs, columns // 3)

    def kernel(*refs):
        attend_kernel(seqs, *refs)

    return pl.pallas_call(
        kernel,
        out_shape=(jax.ShapeDtypeStruct(shape, jnp.bfloat16),) * 2,
        in_specs=[SMEM] + [VMEM] * 3,
        out_specs=(VMEM, VMEM),
        scratch_shapes=[pltpu.VMEM((CORES,) + shape, jnp.bfloat16)],
    )(info, qkv, prefix, gain)


def join_kernel(info_ref, mine, came, out):
    core, half = info_ref[0], mine.shape[-1]
    out[:, :, pl.ds(pl.multiple_of(core * half, HD), half)] = mine[...]
    out[:, :, pl.ds(pl.multiple_of((1 - core) * half, HD), half)] = came[...]


def join(info, mine, came):
    shape = mine.shape[:-1] + (CORES * mine.shape[-1],)
    return pl.pallas_call(
        join_kernel,
        out_shape=jax.ShapeDtypeStruct(shape, mine.dtype),
        in_specs=[SMEM] + [VMEM] * 2,
        out_specs=VMEM,
    )(info, mine, came)


def body(tokens, w_query, w_key, w_value, norm_gain, *, heads):
    seq_count, span_len, shard = tokens.shape
    features = w_query.shape[1]
    half = features // CORES
    rows = seq_count * span_len
    ctx_at = lax.axis_index("ctx")
    core = ctx_at % CORES
    z_at = (ctx_at // CORES) % SIDE
    y_at = ctx_at // (CORES * SIDE)
    second = jnp.where(core == 0, y_at, z_at)
    head_at = lax.axis_index("head")
    is_first = core == 0

    def pair(own, came):
        return jnp.concatenate([jnp.where(is_first, own, came), jnp.where(is_first, came, own)], axis=0)

    low = jnp.concatenate([w[:, :half] for w in (w_query, w_key, w_value)], axis=1)
    high = jnp.concatenate([w[:, half:] for w in (w_query, w_key, w_value)], axis=1)
    came = lax.ppermute(jnp.where(is_first, high, low), "ctx", across())
    chip_rows = pair(jnp.where(is_first, low, high), came)

    natural = tokens.reshape(rows, shard)
    per_y = shard // 2
    turned = natural.reshape(rows, 2, SIDE, per_y // SIDE).transpose(0, 2, 1, 3).reshape(rows, shard)
    came = lax.ppermute(jnp.where(is_first, turned, natural), "ctx", across())
    chip_tokens = pair(jnp.where(is_first, natural, turned), came)
    pieces = [chip_tokens]
    for hop in range(1, heads):
        ring = [(i, (i + hop) % heads) for i in range(heads)]
        pieces.append(lax.ppermute(chip_tokens, "head", ring))

    depth, columns = chip_rows.shape
    copies = jnp.broadcast_to(chip_rows[None], (SIDE, depth, columns))
    block = lax.all_to_all(copies, "ctx", 0, 0, tiled=True, axis_index_groups=first_groups())
    block = block.reshape(SIDE * depth, columns)

    blocks = [block]
    up = down = block
    for hop in range(1, SIDE // 2 + 1):
        up = lax.ppermute(up, "ctx", along_second(1))
        blocks.append(up)
        if hop < SIDE // 2:
            down = lax.ppermute(down, "ctx", along_second(-1))
            blocks.append(down)
    info = call_info(core, second, head_at)
    early = 7
    sums = early_product(info, pieces, blocks[:early])
    qkv, states = late_product(info, pieces, blocks[early:], sums, early, seq_count)

    chips = SIDE * SIDE
    slices = lax.all_to_all(
        states.reshape(chips, -1, HD), "ctx", 0, 0, tiled=True, axis_index_groups=chip_groups()
    )
    prefix = lax.all_to_all(exclusive(slices), "ctx", 0, 0, tiled=True, axis_index_groups=chip_groups())
    gain = jnp.where(is_first, norm_gain[:half], norm_gain[half:]).reshape(1, half)
    mine, other = attend(info, qkv, prefix.reshape(states.shape), gain, seq_count)
    return join(info, mine, lax.ppermute(other, "ctx", across()))


def solution(mesh):
    sizes = dict(mesh.shape)
    in_specs = (P(None, "ctx", "head"), P("ctx", "head"), P("ctx", "head"), P("ctx", "head"), P("head"))

    def step(*operands):
        return body(*operands, heads=sizes["head"])

    return jax.shard_map(step, mesh=mesh, in_specs=in_specs, out_specs=P(None, "ctx", "head"), check_vma=False)
```

```python
import jax
import jax.numpy as jnp
from jax import lax
from jax.experimental import pallas as pl
from jax.experimental.pallas import tpu as pltpu
from jax.sharding import PartitionSpec as P


HD = 128
SIDE = 8
CORES = 2


def index(y, z, core):
    return ((y % SIDE) * SIDE + z % SIDE) * CORES + core


def everyone():
    return [(y, z, core) for y in range(SIDE) for z in range(SIDE) for core in range(CORES)]


def across():
    return [(index(y, z, core), index(y, z, 1 - core)) for y, z, core in everyone()]


def along_second(hop):
    return [
        (index(y, z, core), index(y + hop, z, core) if core == 0 else index(y, z + hop, core))
        for y, z, core in everyone()
    ]


def first_groups():
    groups = [[index(y, z, 0) for z in range(SIDE)] for y in range(SIDE)]
    return groups + [[index(y, z, 1) for y in range(SIDE)] for z in range(SIDE)]


def chip_groups():
    return [[index(y, z, core) for y in range(SIDE) for z in range(SIDE)] for core in range(CORES)]


def block_at(number, second):
    far = (number + 1) // 2
    return jnp.where(number % 2 == 1, second + SIDE - far, second + far) % SIDE


def left_of(info_ref, lhs, number, steps):
    core, second, head_at = info_ref[0], info_ref[1], info_ref[2]
    heads = lhs.shape[0]
    at = block_at(number, second)
    parts = []
    for p in range(steps):
        part = jnp.where(core == 0, at // 2, p)
        hop = (head_at + heads - part) % heads
        lane = jnp.where(core == 0, (at % 2) * steps + p, at)
        parts.append(lhs[hop, :, pl.ds(pl.multiple_of(lane * HD, HD), HD)])
    return parts


def early_kernel(heads, count, info_ref, *refs):
    pieces, blocks = refs[:heads], refs[heads : heads + count]
    total, last, lhs, rhs, lhs_sems, rhs_sems = refs[heads + count :]
    depth, columns = rhs.shape[1:]
    steps, group = depth // HD, 2 * HD
    lhs_copies = [pltpu.make_async_copy(r, lhs.at[i], lhs_sems.at[i]) for i, r in enumerate(pieces)]
    rhs_copies = [pltpu.make_async_copy(r, rhs.at[i], rhs_sems.at[i]) for i, r in enumerate(blocks)]
    for copy in lhs_copies + rhs_copies:
        copy.start()
    for copy in lhs_copies:
        copy.wait()
    for number in range(count, count + last.shape[1] // depth):
        cols = slice((number - count) * depth, (number - count + 1) * depth)
        last[:, cols] = jnp.concatenate(left_of(info_ref, lhs, number, steps), axis=1)
    rhs_copies[0].wait()
    left = jnp.concatenate(left_of(info_ref, lhs, 0, steps), axis=1)
    for g in range(columns // group):
        cols = slice(g * group, (g + 1) * group)
        total[:, cols] = jnp.dot(left, rhs[0, :, cols], preferred_element_type=jnp.float32)

    def two(pair, _):
        number = 2 * pair + 1
        for i in range(2):
            pltpu.make_async_copy(blocks[0], rhs.at[number + i], rhs_sems.at[number + i]).wait()
        left = [part for i in range(2) for part in left_of(info_ref, lhs, number + i, steps)]
        left = jnp.concatenate(left, axis=1)
        for g in range(columns // group):
            cols = slice(g * group, (g + 1) * group)
            right = rhs[pl.ds(number, 2), :, cols].reshape(2 * depth, group)
            total[:, cols] += jnp.dot(left, right, preferred_element_type=jnp.float32)
        return 0

    lax.fori_loop(0, count // 2, two, 0)


def late_kernel(seqs, *refs):
    count = len(refs) - 6
    blocks, (left, sums, qkv, states, rhs, sems) = refs[:count], refs[count:]
    columns = sums.shape[1]
    half, group = columns // 3, 2 * HD
    copies, ends, end = [], [], 0
    for i, block in enumerate(blocks):
        rows = pl.ds(end, block.shape[0])
        copies.append(pltpu.make_async_copy(block, rhs.at[rows], sems.at[i]))
        end += block.shape[0]
        ends.append(end)
    for copy in copies:
        copy.start()
    copies[0].wait()
    first = ends[0]
    for g in range(columns // group):
        cols = slice(g * group, (g + 1) * group)
        sums[:, cols] += jnp.dot(left[:, :first], rhs[:first, cols], preferred_element_type=jnp.float32)
    for copy in copies[1:]:
        copy.wait()
    for g in range(columns // group):
        cols = slice(g * group, (g + 1) * group)
        total = sums[:, cols] + jnp.dot(left[:, first:], rhs[first:, cols], preferred_element_type=jnp.float32)
        if g * group < 2 * half:
            total = total / (1.0 + jnp.exp(-total))
        qkv[:, cols] = total.astype(qkv.dtype)
    span = sums.shape[0] // (CORES * seqs)
    for s in range(seqs):
        for h in range(half // HD):
            acc = jnp.zeros((HD, HD), jnp.float32)
            for c in range(CORES):
                at = pl.ds((c * seqs + s) * span, span)
                key = qkv[at, pl.ds(half + h * HD, HD)]
                value = qkv[at, pl.ds(2 * half + h * HD, HD)]
                acc += lax.dot_general(key, value, (((0,), (0,)), ((), ())), preferred_element_type=jnp.float32)
            states[s, h] = acc


def call_info(core, second, head_at):
    return jnp.stack([core, second, head_at]).astype(jnp.int32)


SMEM = pl.BlockSpec(memory_space=pltpu.SMEM)
ANY = pl.BlockSpec(memory_space=pl.ANY)
VMEM = pl.BlockSpec(memory_space=pltpu.VMEM)


def early_product(info, pieces, blocks, later):
    rows, (depth, columns) = pieces[0].shape[0], blocks[0].shape
    heads, count = len(pieces), len(blocks)

    def kernel(*refs):
        early_kernel(heads, count, *refs)

    return pl.pallas_call(
        kernel,
        out_shape=(
            jax.ShapeDtypeStruct((rows, columns), jnp.float32),
            jax.ShapeDtypeStruct((rows, later * depth), pieces[0].dtype),
        ),
        in_specs=[SMEM] + [ANY] * (heads + count),
        out_specs=(VMEM, VMEM),
        scratch_shapes=[
            pltpu.VMEM((heads,) + pieces[0].shape, pieces[0].dtype),
            pltpu.VMEM((count, depth, columns), blocks[0].dtype),
            pltpu.SemaphoreType.DMA((heads,)),
            pltpu.SemaphoreType.DMA((count,)),
        ],
        cost_estimate=pl.CostEstimate(
            flops=2 * rows * columns * depth * count, bytes_accessed=8 << 20, transcendentals=0
        ),
    )(info, *pieces, *blocks)


def late_product(blocks, left, sums, seqs):
    rows, columns = sums.shape

    def kernel(*refs):
        count = len(blocks)
        sums_ref, total = refs[count + 1], refs[-1]
        total[...] = sums_ref[...]
        late_kernel(seqs, *refs[: count + 1], total, *refs[count + 2 : -1])

    return pl.pallas_call(
        kernel,
        out_shape=(
            jax.ShapeDtypeStruct((rows, columns), jnp.bfloat16),
            jax.ShapeDtypeStruct((seqs, columns // 3 // HD, HD, HD), jnp.float32),
        ),
        in_specs=[ANY] * len(blocks) + [VMEM] * 2,
        out_specs=(VMEM, VMEM),
        scratch_shapes=[
            pltpu.VMEM((left.shape[1], columns), left.dtype),
            pltpu.SemaphoreType.DMA((len(blocks),)),
            pltpu.VMEM((rows, columns), jnp.float32),
        ],
    )(*blocks, left, sums)


def scan_kernel(slices_ref, prefix_ref):
    def one(block, carried):
        prefix_ref[block] = carried.astype(prefix_ref.dtype)
        return carried + slices_ref[block]

    lax.fori_loop(0, slices_ref.shape[0], one, jnp.zeros(slices_ref.shape[1:], jnp.float32), unroll=8)


def exclusive(slices):
    return pl.pallas_call(
        scan_kernel,
        out_shape=jax.ShapeDtypeStruct(slices.shape, jnp.bfloat16),
        in_specs=[VMEM],
        out_specs=VMEM,
    )(slices)


def both_spans(qkv, seqs, s, h, kind):
    half = qkv.shape[1] // 3
    span = qkv.shape[0] // (CORES * seqs)
    lanes = pl.ds(kind * half + h * HD, HD)
    return jnp.concatenate([qkv[pl.ds((c * seqs + s) * span, span), lanes] for c in range(CORES)], axis=0)


def local_kernel(seqs, qkv, out):
    both = qkv.shape[0] // seqs
    ahead = lax.broadcasted_iota(jnp.int32, (both, both), 0)
    causal = ahead >= lax.broadcasted_iota(jnp.int32, (both, both), 1)
    for s in range(seqs):
        for h in range(out.shape[1]):
            query, key, value = (both_spans(qkv, seqs, s, h, kind) for kind in range(3))
            scores = lax.dot_general(query, key, (((1,), (1,)), ((), ())), preferred_element_type=jnp.float32)
            masked = jnp.where(causal, scores, 0.0).astype(jnp.bfloat16)
            out[s, h] = jnp.dot(masked, value, preferred_element_type=jnp.float32)


def local_part(qkv, seqs):
    rows, columns = qkv.shape

    def kernel(*refs):
        local_kernel(seqs, *refs)

    return pl.pallas_call(
        kernel,
        out_shape=jax.ShapeDtypeStruct((seqs, columns // 3 // HD, rows // seqs, HD), jnp.float32),
        in_specs=[VMEM],
        out_specs=VMEM,
    )(qkv)


def attend_kernel(seqs, info_ref, qkv, local, prefix, gain, whole, other, spans):
    span = qkv.shape[0] // (CORES * seqs)
    for s in range(seqs):
        for h in range(local.shape[1]):
            query = both_spans(qkv, seqs, s, h, 0)
            total = local[s, h] + jnp.dot(query, prefix[s, h], preferred_element_type=jnp.float32)
            scale_inv = lax.rsqrt(jnp.mean(total * total, axis=-1, keepdims=True) + 1e-06)
            normed = (total * scale_inv * gain[:, pl.ds(h * HD, HD)]).astype(whole.dtype)
            for c in range(CORES):
                spans[c, s, :, pl.ds(h * HD, HD)] = normed[c * span : (c + 1) * span]
    core, half = info_ref[0], other.shape[-1]
    whole[:, :, pl.ds(pl.multiple_of(core * half, HD), half)] = spans[core]
    other[...] = spans[1 - core]


def attend(info, qkv, local, prefix, gain, seqs):
    rows, columns = qkv.shape
    shape = (seqs, rows // CORES // seqs, columns // 3)

    def kernel(*refs):
        attend_kernel(seqs, *refs)

    return pl.pallas_call(
        kernel,
        out_shape=(
            jax.ShapeDtypeStruct(shape[:-1] + (CORES * shape[-1],), jnp.bfloat16),
            jax.ShapeDtypeStruct(shape, jnp.bfloat16),
        ),
        in_specs=[SMEM] + [VMEM] * 4,
        out_specs=(VMEM, VMEM),
        scratch_shapes=[pltpu.VMEM((CORES,) + shape, jnp.bfloat16)],
    )(info, qkv, local, prefix, gain)


def body(tokens, w_query, w_key, w_value, norm_gain, *, heads):
    seq_count, span_len, shard = tokens.shape
    features = w_query.shape[1]
    half = features // CORES
    rows = seq_count * span_len
    ctx_at = lax.axis_index("ctx")
    core = ctx_at % CORES
    z_at = (ctx_at // CORES) % SIDE
    y_at = ctx_at // (CORES * SIDE)
    second = jnp.where(core == 0, y_at, z_at)
    head_at = lax.axis_index("head")
    is_first = core == 0

    def pair(own, came):
        return jnp.concatenate([jnp.where(is_first, own, came), jnp.where(is_first, came, own)], axis=0)

    low = jnp.concatenate([w[:, :half] for w in (w_query, w_key, w_value)], axis=1)
    high = jnp.concatenate([w[:, half:] for w in (w_query, w_key, w_value)], axis=1)
    halves = [jnp.where(is_first, w[:, :half], w[:, half:]) for w in (w_query, w_key, w_value)]
    kept = jnp.concatenate(halves, axis=1)
    came = lax.ppermute(jnp.where(is_first, high, low), "ctx", across())
    chip_rows = pair(kept, came)

    natural = tokens.reshape(rows, shard)
    per_y = shard // 2
    turned = natural.reshape(rows, 2, SIDE, per_y // SIDE).transpose(0, 2, 1, 3).reshape(rows, shard)
    came = lax.ppermute(jnp.where(is_first, turned, natural), "ctx", across())
    chip_tokens = pair(jnp.where(is_first, natural, turned), came)
    pieces = [chip_tokens]
    for hop in range(1, heads):
        ring = [(i, (i + hop) % heads) for i in range(heads)]
        pieces.append(lax.ppermute(chip_tokens, "head", ring))

    depth, columns = chip_rows.shape
    copies = jnp.broadcast_to(chip_rows[None], (SIDE, depth, columns))
    block = lax.all_to_all(copies, "ctx", 0, 0, tiled=True, axis_index_groups=first_groups())
    block = block.reshape(SIDE * depth, columns)

    blocks = [block]
    up = down = block
    for _ in range(1, SIDE // 2 - 1):
        up = lax.ppermute(up, "ctx", along_second(1))
        down = lax.ppermute(down, "ctx", along_second(-1))
        blocks += [up, down]
    far_up = lax.ppermute(up, "ctx", along_second(1))
    far_down = lax.ppermute(down, "ctx", along_second(-1))
    deep = block.shape[0] // 2
    top = lax.ppermute(up[:deep], "ctx", along_second(2))
    bottom = lax.ppermute(down[deep:], "ctx", along_second(-2))
    info = call_info(core, second, head_at)
    sums, left = early_product(info, pieces, blocks, SIDE - len(blocks))
    qkv, states = late_product([far_up, far_down, top, bottom], left, sums, seq_count)

    chips = SIDE * SIDE
    slices = lax.all_to_all(
        states.reshape(chips, -1, HD), "ctx", 0, 0, tiled=True, axis_index_groups=chip_groups()
    )
    local = local_part(qkv, seq_count)
    prefix = lax.all_to_all(exclusive(slices), "ctx", 0, 0, tiled=True, axis_index_groups=chip_groups())
    gain = jnp.where(is_first, norm_gain[:half], norm_gain[half:]).reshape(1, half)
    whole, other = attend(info, qkv, local, prefix.reshape(states.shape), gain, seq_count)
    came = lax.ppermute(other, "ctx", across())
    return lax.dynamic_update_slice(whole, came, (0, 0, (1 - core) * half))


def solution(mesh):
    sizes = dict(mesh.shape)
    in_specs = (P(None, "ctx", "head"), P("ctx", "head"), P("ctx", "head"), P("ctx", "head"), P("head"))

    def step(*operands):
        return body(*operands, heads=sizes["head"])

    return jax.shard_map(step, mesh=mesh, in_specs=in_specs, out_specs=P(None, "ctx", "head"), check_vma=False)
```

```python
import jax
import jax.numpy as jnp
from jax import lax
from jax.experimental import pallas as pl
from jax.experimental.pallas import tpu as pltpu
from jax.sharding import PartitionSpec as P


HD = 128
SIDE = 8
CORES = 2


def index(y, z, core):
    return ((y % SIDE) * SIDE + z % SIDE) * CORES + core


def everyone():
    return [(y, z, core) for y in range(SIDE) for z in range(SIDE) for core in range(CORES)]


def across():
    return [(index(y, z, core), index(y, z, 1 - core)) for y, z, core in everyone()]


def along_second(hop):
    return [
        (index(y, z, core), index(y + hop, z, core) if core == 0 else index(y, z + hop, core))
        for y, z, core in everyone()
    ]


def first_groups():
    groups = [[index(y, z, 0) for z in range(SIDE)] for y in range(SIDE)]
    return groups + [[index(y, z, 1) for y in range(SIDE)] for z in range(SIDE)]


def chip_groups():
    return [[index(y, z, core) for y in range(SIDE) for z in range(SIDE)] for core in range(CORES)]


def block_at(number, second):
    far = (number + 1) // 2
    return jnp.where(number % 2 == 1, second + SIDE - far, second + far) % SIDE


def left_of(info_ref, lhs, number, steps):
    core, second, head_at = info_ref[0], info_ref[1], info_ref[2]
    heads = lhs.shape[0]
    at = block_at(number, second)
    parts = []
    for p in range(steps):
        part = jnp.where(core == 0, at // 2, p)
        hop = (head_at + heads - part) % heads
        lane = jnp.where(core == 0, (at % 2) * steps + p, at)
        parts.append(lhs[hop, :, pl.ds(pl.multiple_of(lane * HD, HD), HD)])
    return parts


def early_kernel(heads, count, info_ref, *refs):
    pieces, blocks = refs[:heads], refs[heads : heads + count]
    total, last, lhs, rhs, lhs_sems, rhs_sems = refs[heads + count :]
    depth, columns = rhs.shape[1:]
    steps, group = depth // HD, 2 * HD
    lhs_copies = [pltpu.make_async_copy(r, lhs.at[i], lhs_sems.at[i]) for i, r in enumerate(pieces)]
    rhs_copies = [pltpu.make_async_copy(r, rhs.at[i], rhs_sems.at[i]) for i, r in enumerate(blocks)]
    for copy in lhs_copies + rhs_copies:
        copy.start()
    for copy in lhs_copies:
        copy.wait()
    for number in range(count, count + last.shape[1] // depth):
        cols = slice((number - count) * depth, (number - count + 1) * depth)
        last[:, cols] = jnp.concatenate(left_of(info_ref, lhs, number, steps), axis=1)
    rhs_copies[0].wait()
    left = jnp.concatenate(left_of(info_ref, lhs, 0, steps), axis=1)
    for g in range(columns // group):
        cols = slice(g * group, (g + 1) * group)
        total[:, cols] = jnp.dot(left, rhs[0, :, cols], preferred_element_type=jnp.float32)

    def two(pair, _):
        number = 2 * pair + 1
        for i in range(2):
            pltpu.make_async_copy(blocks[0], rhs.at[number + i], rhs_sems.at[number + i]).wait()
        left = [part for i in range(2) for part in left_of(info_ref, lhs, number + i, steps)]
        left = jnp.concatenate(left, axis=1)
        for g in range(columns // group):
            cols = slice(g * group, (g + 1) * group)
            right = rhs[pl.ds(number, 2), :, cols].reshape(2 * depth, group)
            total[:, cols] += jnp.dot(left, right, preferred_element_type=jnp.float32)
        return 0

    lax.fori_loop(0, count // 2, two, 0, unroll=True)


def late_kernel(seqs, *refs):
    count = len(refs) - 7
    blocks, (left, sums, qkv, states, rhs, sems, total_ref) = refs[:count], refs[count:]
    columns = sums.shape[1]
    half, group = columns // 3, 2 * HD
    copies, ends, end = [], [], 0
    for i, block in enumerate(blocks):
        rows = pl.ds(end, block.shape[0])
        copies.append(pltpu.make_async_copy(block, rhs.at[rows], sems.at[i]))
        end += block.shape[0]
        ends.append(end)
    for copy in copies:
        copy.start()
    copies[0].wait()
    first = ends[0]
    for g in range(columns // group):
        cols = slice(g * group, (g + 1) * group)
        part = jnp.dot(left[:, :first], rhs[:first, cols], preferred_element_type=jnp.float32)
        total_ref[:, cols] = sums[:, cols] + part
    for copy in copies[1:]:
        copy.wait()
    for g in range(columns // group):
        cols = slice(g * group, (g + 1) * group)
        total = total_ref[:, cols] + jnp.dot(left[:, first:], rhs[first:, cols], preferred_element_type=jnp.float32)
        if g * group < 2 * half:
            total = total / (1.0 + jnp.exp(-total))
        qkv[:, cols] = total.astype(qkv.dtype)
    span = sums.shape[0] // (CORES * seqs)
    for s in range(seqs):
        for h in range(half // HD):
            acc = jnp.zeros((HD, HD), jnp.float32)
            for c in range(CORES):
                at = pl.ds((c * seqs + s) * span, span)
                key = qkv[at, pl.ds(half + h * HD, HD)]
                value = qkv[at, pl.ds(2 * half + h * HD, HD)]
                acc += lax.dot_general(key, value, (((0,), (0,)), ((), ())), preferred_element_type=jnp.float32)
            states[s, h] = acc


def call_info(core, second, head_at):
    return jnp.stack([core, second, head_at]).astype(jnp.int32)


SMEM = pl.BlockSpec(memory_space=pltpu.SMEM)
ANY = pl.BlockSpec(memory_space=pl.ANY)
VMEM = pl.BlockSpec(memory_space=pltpu.VMEM)


def early_product(info, pieces, blocks, later):
    rows, (depth, columns) = pieces[0].shape[0], blocks[0].shape
    heads, count = len(pieces), len(blocks)

    def kernel(*refs):
        early_kernel(heads, count, *refs)

    return pl.pallas_call(
        kernel,
        out_shape=(
            jax.ShapeDtypeStruct((rows, columns), jnp.float32),
            jax.ShapeDtypeStruct((rows, later * depth), pieces[0].dtype),
        ),
        in_specs=[SMEM] + [ANY] * (heads + count),
        out_specs=(VMEM, VMEM),
        scratch_shapes=[
            pltpu.VMEM((heads,) + pieces[0].shape, pieces[0].dtype),
            pltpu.VMEM((count, depth, columns), blocks[0].dtype),
            pltpu.SemaphoreType.DMA((heads,)),
            pltpu.SemaphoreType.DMA((count,)),
        ],
        cost_estimate=pl.CostEstimate(
            flops=2 * rows * columns * depth * count, bytes_accessed=8 << 20, transcendentals=0
        ),
    )(info, *pieces, *blocks)


def late_product(blocks, left, sums, seqs):
    rows, columns = sums.shape

    def kernel(*refs):
        late_kernel(seqs, *refs)

    return pl.pallas_call(
        kernel,
        out_shape=(
            jax.ShapeDtypeStruct((rows, columns), jnp.bfloat16),
            jax.ShapeDtypeStruct((seqs, columns // 3 // HD, HD, HD), jnp.float32),
        ),
        in_specs=[ANY] * len(blocks) + [VMEM] * 2,
        out_specs=(VMEM, VMEM),
        scratch_shapes=[
            pltpu.VMEM((left.shape[1], columns), left.dtype),
            pltpu.SemaphoreType.DMA((len(blocks),)),
            pltpu.VMEM((rows, columns), jnp.float32),
        ],
    )(*blocks, left, sums)


def scan_kernel(slices_ref, prefix_ref):
    def one(block, carried):
        prefix_ref[block] = carried.astype(prefix_ref.dtype)
        return carried + slices_ref[block]

    lax.fori_loop(0, slices_ref.shape[0], one, jnp.zeros(slices_ref.shape[1:], jnp.float32), unroll=8)


def exclusive(slices):
    return pl.pallas_call(
        scan_kernel,
        out_shape=jax.ShapeDtypeStruct(slices.shape, jnp.bfloat16),
        in_specs=[VMEM],
        out_specs=VMEM,
    )(slices)


def both_spans(qkv, seqs, s, h, kind):
    half = qkv.shape[1] // 3
    span = qkv.shape[0] // (CORES * seqs)
    lanes = pl.ds(kind * half + h * HD, HD)
    return jnp.concatenate([qkv[pl.ds((c * seqs + s) * span, span), lanes] for c in range(CORES)], axis=0)


def local_kernel(seqs, qkv, out):
    both = qkv.shape[0] // seqs
    ahead = lax.broadcasted_iota(jnp.int32, (both, both), 0)
    causal = ahead >= lax.broadcasted_iota(jnp.int32, (both, both), 1)
    for s in range(seqs):
        for h in range(out.shape[1]):
            query, key, value = (both_spans(qkv, seqs, s, h, kind) for kind in range(3))
            scores = lax.dot_general(query, key, (((1,), (1,)), ((), ())), preferred_element_type=jnp.float32)
            masked = jnp.where(causal, scores, 0.0).astype(jnp.bfloat16)
            out[s, h] = jnp.dot(masked, value, preferred_element_type=jnp.float32)


def local_part(qkv, seqs):
    rows, columns = qkv.shape

    def kernel(*refs):
        local_kernel(seqs, *refs)

    return pl.pallas_call(
        kernel,
        out_shape=jax.ShapeDtypeStruct((seqs, columns // 3 // HD, rows // seqs, HD), jnp.float32),
        in_specs=[VMEM],
        out_specs=VMEM,
    )(qkv)


def attend_kernel(seqs, info_ref, qkv, local, prefix, gain, whole, other, spans):
    span = qkv.shape[0] // (CORES * seqs)
    for s in range(seqs):
        for h in range(local.shape[1]):
            query = both_spans(qkv, seqs, s, h, 0)
            total = local[s, h] + jnp.dot(query, prefix[s, h], preferred_element_type=jnp.float32)
            scale_inv = lax.rsqrt(jnp.mean(total * total, axis=-1, keepdims=True) + 1e-06)
            normed = (total * scale_inv * gain[:, pl.ds(h * HD, HD)]).astype(whole.dtype)
            for c in range(CORES):
                spans[c, s, :, pl.ds(h * HD, HD)] = normed[c * span : (c + 1) * span]
    core, half = info_ref[0], other.shape[-1]
    whole[:, :, pl.ds(pl.multiple_of(core * half, HD), half)] = spans[core]
    other[...] = spans[1 - core]


def attend(info, qkv, local, prefix, gain, seqs):
    rows, columns = qkv.shape
    shape = (seqs, rows // CORES // seqs, columns // 3)

    def kernel(*refs):
        attend_kernel(seqs, *refs)

    return pl.pallas_call(
        kernel,
        out_shape=(
            jax.ShapeDtypeStruct(shape[:-1] + (CORES * shape[-1],), jnp.bfloat16),
            jax.ShapeDtypeStruct(shape, jnp.bfloat16),
        ),
        in_specs=[SMEM] + [VMEM] * 4,
        out_specs=(VMEM, VMEM),
        scratch_shapes=[pltpu.VMEM((CORES,) + shape, jnp.bfloat16)],
    )(info, qkv, local, prefix, gain)


def body(tokens, w_query, w_key, w_value, norm_gain, *, heads):
    seq_count, span_len, shard = tokens.shape
    features = w_query.shape[1]
    half = features // CORES
    rows = seq_count * span_len
    ctx_at = lax.axis_index("ctx")
    core = ctx_at % CORES
    z_at = (ctx_at // CORES) % SIDE
    y_at = ctx_at // (CORES * SIDE)
    second = jnp.where(core == 0, y_at, z_at)
    head_at = lax.axis_index("head")
    is_first = core == 0

    def pair(own, came):
        return jnp.concatenate([jnp.where(is_first, own, came), jnp.where(is_first, came, own)], axis=0)

    low = jnp.concatenate([w[:, :half] for w in (w_query, w_key, w_value)], axis=1)
    high = jnp.concatenate([w[:, half:] for w in (w_query, w_key, w_value)], axis=1)
    halves = [jnp.where(is_first, w[:, :half], w[:, half:]) for w in (w_query, w_key, w_value)]
    kept = jnp.concatenate(halves, axis=1)
    came = lax.ppermute(jnp.where(is_first, high, low), "ctx", across())
    chip_rows = pair(kept, came)

    natural = tokens.reshape(rows, shard)
    per_y = shard // 2
    turned = natural.reshape(rows, 2, SIDE, per_y // SIDE).transpose(0, 2, 1, 3).reshape(rows, shard)
    came = lax.ppermute(jnp.where(is_first, turned, natural), "ctx", across())
    chip_tokens = pair(jnp.where(is_first, natural, turned), came)
    pieces = [chip_tokens]
    for hop in range(1, heads):
        ring = [(i, (i + hop) % heads) for i in range(heads)]
        pieces.append(lax.ppermute(chip_tokens, "head", ring))

    depth, columns = chip_rows.shape
    copies = jnp.broadcast_to(chip_rows[None], (SIDE, depth, columns))
    block = lax.all_to_all(copies, "ctx", 0, 0, tiled=True, axis_index_groups=first_groups())
    block = block.reshape(SIDE * depth, columns)

    blocks = [block]
    up = down = block
    for _ in range(1, SIDE // 2 - 1):
        up = lax.ppermute(up, "ctx", along_second(1))
        down = lax.ppermute(down, "ctx", along_second(-1))
        blocks += [up, down]
    far_up = lax.ppermute(up, "ctx", along_second(1))
    far_down = lax.ppermute(down, "ctx", along_second(-1))
    deep = block.shape[0] // 2
    top = lax.ppermute(up[:deep], "ctx", along_second(2))
    bottom = lax.ppermute(down[deep:], "ctx", along_second(-2))
    info = call_info(core, second, head_at)
    sums, left = early_product(info, pieces, blocks, SIDE - len(blocks))
    qkv, states = late_product([far_up, far_down, top, bottom], left, sums, seq_count)

    chips = SIDE * SIDE
    slices = lax.all_to_all(
        states.reshape(chips, -1, HD), "ctx", 0, 0, tiled=True, axis_index_groups=chip_groups()
    )
    local = local_part(qkv, seq_count)
    prefix = lax.all_to_all(exclusive(slices), "ctx", 0, 0, tiled=True, axis_index_groups=chip_groups())
    gain = jnp.where(is_first, norm_gain[:half], norm_gain[half:]).reshape(1, half)
    whole, other = attend(info, qkv, local, prefix.reshape(states.shape), gain, seq_count)
    came = lax.ppermute(other, "ctx", across())
    return lax.dynamic_update_slice(whole, came, (0, 0, (1 - core) * half))


def solution(mesh):
    sizes = dict(mesh.shape)
    in_specs = (P(None, "ctx", "head"), P("ctx", "head"), P("ctx", "head"), P("ctx", "head"), P("head"))

    def step(*operands):
        return body(*operands, heads=sizes["head"])

    return jax.shard_map(step, mesh=mesh, in_specs=in_specs, out_specs=P(None, "ctx", "head"), check_vma=False)
```
